32 devices in a mesh: dp: 8 (over z, x), branch: 4 (over y, core).
Axes of the slice: x: 2, y: 2, z: 4, core: 2. Of those that a mesh axis runs over, the one named last changes fastest.
Arguments:
- inputs: bfloat16 [16, 512, 2048], P('dp', 'branch'), may hold values from -6 to 6
- segments: int32 [16, 512], P('dp'), may hold values from 0 to 4, as said below
- out_grad: bfloat16 [16, 512, 2048], P('dp', 'branch'), may hold values from -6 to 6
- layer_params: float32 [3, 2048], replicated, may hold values from -0.5 to 2.4
- attend_weight: float32 [3, 2048, 2048], P(None, 'dp', 'branch'), may hold values from -0.125 to 0.125
- attend_bias: float32 [3, 2048], P(None, ('branch', 'dp')), may hold values from -1.5 to 1.5
- output_weight: float32 [2048, 2048], P('branch', 'dp'), may hold values from -0.75 to 0.75
- expand_weight: float32 [2048, 8192], P('dp', 'branch'), may hold values from -0.125 to 0.125
- expand_bias: float32 [8192], P(('branch', 'dp')), may hold values from -1.5 to 1.5
- shrink_weight: float32 [8192, 2048], P('branch', 'dp'), may hold values from -0.0625 to 0.0625
- mean_layer: float32 [3, 2048], replicated, may hold values from -10 to 10
- mean_attend_weight: float32 [3, 2048, 2048], P(None, 'dp', 'branch'), may hold values from -6 to 6
- mean_attend_bias: float32 [3, 2048], P(None, ('branch', 'dp')), may hold values from -6 to 6
- mean_output_weight: float32 [2048, 2048], P('branch', 'dp'), may hold values from -6 to 6
- mean_expand_weight: float32 [2048, 8192], P('dp', 'branch'), may hold values from -6 to 6
- mean_expand_bias: float32 [8192], P(('branch', 'dp')), may hold values from -6 to 6
- mean_shrink_weight: float32 [8192, 2048], P('branch', 'dp'), may hold values from -6 to 6
- square_layer: float32 [3, 2048], replicated, may hold values from 4 to 16
- square_attend_weight: float32 [3, 2048, 2048], P(None, 'dp', 'branch'), may hold values from 1 to 4
- square_attend_bias: float32 [3, 2048], P(None, ('branch', 'dp')), may hold values from 1 to 4
- square_output_weight: float32 [2048, 2048], P('branch', 'dp'), may hold values from 1 to 4
- square_expand_weight: float32 [2048, 8192], P('dp', 'branch'), may hold values from 1 to 4
- square_expand_bias: float32 [8192], P(('branch', 'dp')), may hold values from 1 to 4
- square_shrink_weight: float32 [8192, 2048], P('branch', 'dp'), may hold values from 1 to 4
Outputs:
- block_output: bfloat16 [16, 512, 2048], P('dp', 'branch')
- grad_inputs: bfloat16 [16, 512, 2048], P('dp', 'branch')
- grad_norm: float32 [1], replicated
- next_layer: float32 [3, 2048], replicated
- next_attend_weight: float32 [3, 2048, 2048], P(None, 'dp', 'branch')
- next_attend_bias: float32 [3, 2048], P(None, ('branch', 'dp'))
- next_output_weight: float32 [2048, 2048], P('branch', 'dp')
- next_expand_weight: float32 [2048, 8192], P('dp', 'branch')
- next_expand_bias: float32 [8192], P(('branch', 'dp'))
- next_shrink_weight: float32 [8192, 2048], P('branch', 'dp')
- next_mean_layer: float32 [3, 2048], replicated
- next_mean_attend_weight: float32 [3, 2048, 2048], P(None, 'dp', 'branch')
- next_mean_attend_bias: float32 [3, 2048], P(None, ('branch', 'dp'))
- next_mean_output_weight: float32 [2048, 2048], P('branch', 'dp')
- next_mean_expand_weight: float32 [2048, 8192], P('dp', 'branch')
- next_mean_expand_bias: float32 [8192], P(('branch', 'dp'))
- next_mean_shrink_weight: float32 [8192, 2048], P('branch', 'dp')
- next_square_layer: float32 [3, 2048], replicated
- next_square_attend_weight: float32 [3, 2048, 2048], P(None, 'dp', 'branch')
- next_square_attend_bias: float32 [3, 2048], P(None, ('branch', 'dp'))
- next_square_output_weight: float32 [2048, 2048], P('branch', 'dp')
- next_square_expand_weight: float32 [2048, 8192], P('dp', 'branch')
- next_square_expand_bias: float32 [8192], P(('branch', 'dp'))
- next_square_shrink_weight: float32 [8192, 2048], P('branch', 'dp')
- copy_attend_weight: bfloat16 [3, 2048, 2048], P(None, 'dp', 'branch')
- copy_output_weight: bfloat16 [2048, 2048], P('branch', 'dp')
- copy_expand_weight: bfloat16 [2048, 8192], P('dp', 'branch')
- copy_shrink_weight: bfloat16 [8192, 2048], P('branch', 'dp')
The draws below stay inside these ranges and needn't reach their ends.
Inputs may be any that keep to these rules, and one draw needn't show every extreme that they name: `segments`: in every row the document numbers start at 0, never fall from token to token; each document holds 1 to 448 tokens, and one document in each row holds exactly 448.
All inputs are finite; a program needn't handle non-finite values.
Results may differ from the reference program's by a relative error of at most 0.012.
The reference program's roundings to bfloat16 on the way count: a program that leaves them out, or rounds other values in their place, can miss the bound.
Values may be sent and summed in bfloat16 or wider, within the bound.
A program may use at most 256 MiB of HBM per device.

```python
import math
import jax
import jax.numpy as jnp
from jax import lax

D = 2048
HEADS = 32
HEAD_DIM = 64
ROT = 32
FF = 8192
ROW_LEN = 512
STEP = 3
BATCH = 16


def draw_layer_params(key, part):
    first, second, third = jax.random.split(jax.random.fold_in(key, 17), 3)
    ramp = 3.0 ** (jnp.arange(D, dtype=jnp.float32) / D - 0.5)
    gain = ramp * jnp.exp(jax.random.uniform(first, (D,), jnp.float32, -0.3, 0.3))
    shift = jax.random.uniform(second, (D,), jnp.float32, -0.5, 0.5)
    out_bias = jax.random.uniform(third, (D,), jnp.float32, -0.5, 0.5)
    return jnp.stack([gain, shift, out_bias]).astype(jnp.float32)


def draw_segments(key, part):
    first, second, third = jax.random.split(jax.random.fold_in(key, 29), 3)
    longest = ROW_LEN - ROW_LEN // 8
    begin = jax.random.randint(first, (BATCH, 1), 0, ROW_LEN - longest, dtype=jnp.int32)
    early = jax.random.randint(second, (BATCH, 1), 0, begin + 1, dtype=jnp.int32)
    late = jax.random.randint(third, (BATCH, 1), begin + longest, ROW_LEN, dtype=jnp.int32)
    places = jnp.arange(ROW_LEN, dtype=jnp.int32)[None, :]
    numbers = (places >= early).astype(jnp.int32) + (places >= begin).astype(jnp.int32) + (places >= begin + longest).astype(jnp.int32) + (places >= late).astype(jnp.int32)
    return (numbers - numbers[:, :1]).astype(jnp.int32)


def block_scale(key, shape, cuts, least, largest):
    level = 1.0
    for axis_at, parts in cuts:
        heights = jax.random.uniform(jax.random.fold_in(jax.random.fold_in(key, 6), axis_at), (parts,), jnp.float32, least / len(cuts), largest / len(cuts))
        level = level * jnp.repeat(jnp.exp(heights), shape[axis_at] // parts).reshape((-1,) + (1,) * (len(shape) - 1 - axis_at))
    return level


def noise(stream_key, shape, scale, reach, cuts=(), kind=jnp.bfloat16):
    values = jax.random.normal(stream_key, shape, jnp.float32) * scale
    if len(cuts) > 0:
        values = block_scale(stream_key, shape, cuts, -0.22, 0.18) * values
    return jnp.clip(values, min=-reach, max=reach).astype(kind)


def setup_inputs(seed: int = 0) -> dict:
    key_list = jax.random.split(jax.random.key(seed), 25)
    inputs = noise(key_list[0], (BATCH, ROW_LEN, D), 1.0, 6.0, ((0, 8), (1, 4)))
    segments = draw_segments(jax.random.fold_in(key_list[24], 71), 0)
    out_grad = noise(key_list[2], (BATCH, ROW_LEN, D), 1.0, 6.0, ((0, 8), (1, 4)))
    layer_params = draw_layer_params(jax.random.fold_in(key_list[24], 71), 0)
    attend_weight = noise(key_list[4], (3, D, D), D ** -0.5, 0.125, ((1, 8), (2, 4)), jnp.float32)
    attend_bias = noise(key_list[5], (3, D), 0.3, 1.5, ((1, 32),), jnp.float32)
    output_weight = noise(key_list[6], (D, D), (D // 32) ** -0.5, 0.75, ((0, 4), (1, 8)), jnp.float32)
    expand_weight = noise(key_list[7], (D, FF), D ** -0.5, 0.125, ((0, 8), (1, 4)), jnp.float32)
    expand_bias = noise(key_list[8], (FF,), 0.3, 1.5, ((0, 32),), jnp.float32)
    shrink_weight = noise(key_list[9], (FF, D), FF ** -0.5, 0.0625, ((0, 4), (1, 8)), jnp.float32)
    mean_layer = noise(key_list[10], (3, D), 2.0, 10.0, (), jnp.float32)
    mean_attend_weight = noise(key_list[11], (3, D, D), 1.0, 6.0, ((1, 8), (2, 4)), jnp.float32)
    mean_attend_bias = noise(key_list[12], (3, D), 1.0, 6.0, ((1, 32),), jnp.float32)
    mean_output_weight = noise(key_list[13], (D, D), 1.0, 6.0, ((0, 4), (1, 8)), jnp.float32)
    mean_expand_weight = noise(key_list[14], (D, FF), 1.0, 6.0, ((0, 8), (1, 4)), jnp.float32)
    mean_expand_bias = noise(key_list[15], (FF,), 1.0, 6.0, ((0, 32),), jnp.float32)
    mean_shrink_weight = noise(key_list[16], (FF, D), 1.0, 6.0, ((0, 4), (1, 8)), jnp.float32)
    square_layer = jnp.clip(jnp.exp(jax.random.uniform(key_list[17], (3, D), jnp.float32, math.log(4.0), math.log(16.0))), 4.0, 16.0)
    square_attend_weight = jnp.clip(jnp.exp(math.log(4.0) - 1.3862944 * jax.random.uniform(key_list[18], (3, D, D), jnp.float32) ** block_scale(key_list[18], (3, D, D), ((1, 8), (2, 4)), -0.2, 0.2)), 1.0, 4.0)
    square_attend_bias = jnp.clip(jnp.exp(math.log(4.0) - 1.3862944 * jax.random.uniform(key_list[19], (3, D), jnp.float32) ** block_scale(key_list[19], (3, D), ((1, 32),), -0.2, 0.2)), 1.0, 4.0)
    square_output_weight = jnp.clip(jnp.exp(math.log(4.0) - 1.3862944 * jax.random.uniform(key_list[20], (D, D), jnp.float32) ** block_scale(key_list[20], (D, D), ((0, 4), (1, 8)), -0.2, 0.2)), 1.0, 4.0)
    square_expand_weight = jnp.clip(jnp.exp(math.log(4.0) - 1.3862944 * jax.random.uniform(key_list[21], (D, FF), jnp.float32) ** block_scale(key_list[21], (D, FF), ((0, 8), (1, 4)), -0.2, 0.2)), 1.0, 4.0)
    square_expand_bias = jnp.clip(jnp.exp(math.log(4.0) - 1.3862944 * jax.random.uniform(key_list[22], (FF,), jnp.float32) ** block_scale(key_list[22], (FF,), ((0, 32),), -0.2, 0.2)), 1.0, 4.0)
    square_shrink_weight = jnp.clip(jnp.exp(math.log(4.0) - 1.3862944 * jax.random.uniform(key_list[23], (FF, D), jnp.float32) ** block_scale(key_list[23], (FF, D), ((0, 4), (1, 8)), -0.2, 0.2)), 1.0, 4.0)
    return {"inputs": inputs, "segments": segments, "out_grad": out_grad, "layer_params": layer_params, "attend_weight": attend_weight, "attend_bias": attend_bias, "output_weight": output_weight, "expand_weight": expand_weight, "expand_bias": expand_bias, "shrink_weight": shrink_weight, "mean_layer": mean_layer, "mean_attend_weight": mean_attend_weight, "mean_attend_bias": mean_attend_bias, "mean_output_weight": mean_output_weight, "mean_expand_weight": mean_expand_weight, "mean_expand_bias": mean_expand_bias, "mean_shrink_weight": mean_shrink_weight, "square_layer": square_layer, "square_attend_weight": square_attend_weight, "square_attend_bias": square_attend_bias, "square_output_weight": square_output_weight, "square_expand_weight": square_expand_weight, "square_expand_bias": square_expand_bias, "square_shrink_weight": square_shrink_weight}


EPS_NORM = 1e-05
ROPE_BASE = 10000.0
BETA_ONE = 0.5
BETA_TWO = 0.5
ADAM_EPS = 1e-08
DECAY = 0.1
MATRIX_RATE = 0.03
VECTOR_RATE = 0.3
MASKED = -1e+30
HIGH = lax.Precision.HIGHEST

@jax.custom_vjp
def low(v):
    return lax.optimization_barrier(v.astype(jnp.bfloat16)).astype(jnp.float32)

@jax.custom_vjp
def low_back(v):
    return v

def low_keep(v):
    return (low(v), None)

def low_pass(kept, grad):
    return (grad,)

def back_keep(v):
    return (v, None)

def back_low(kept, grad):
    return (low(grad),)
low.defvjp(low_keep, low_pass)
low_back.defvjp(back_keep, back_low)

def gelu_tanh(value):
    return 0.5 * value * (1.0 + jnp.tanh(0.7978845608028654 * (value + 0.044715 * value * value * value)))

def doc_positions(segments):
    length = segments.shape[-1]
    places = jnp.arange(length, dtype=jnp.int32)
    before = jnp.concatenate([segments[..., :1] - 1, segments[..., :-1]], axis=-1)
    starts = jnp.where(segments != before, places, 0).astype(jnp.int32)
    starts = lax.cummax(starts, axis=segments.ndim - 1)
    return (places - starts).astype(jnp.int32)

def rotary_tables(positions):
    half = ROT // 2
    freq = ROPE_BASE ** (-(jnp.arange(half, dtype=jnp.float32) * 2.0) / ROT)
    angle = positions.astype(jnp.float32)[..., None] * freq
    return (jnp.cos(angle), jnp.sin(angle))

def rotate(values, cosine, sine):
    half = ROT // 2
    first = values[..., :half]
    second = values[..., half:ROT]
    cosine = cosine[..., None, :]
    sine = sine[..., None, :]
    return jnp.concatenate([first * cosine - second * sine, second * cosine + first * sine, values[..., ROT:]], axis=-1)

def layer(params, rows, cosine, sine, allowed):
    layer_params, attend_weight, attend_bias, output_weight, expand_weight, expand_bias, shrink_weight = params
    groups = rows.shape[0]
    length = rows.shape[1]
    center = rows - lax.optimization_barrier(jnp.mean(rows, -1, keepdims=True))
    normal = center * lax.rsqrt(lax.optimization_barrier(jnp.mean(center * center, -1, keepdims=True)) + EPS_NORM)
    normed = low(normal * layer_params[0] + layer_params[1])
    proj = jnp.einsum('gld,cde->cgle', normed, low(attend_weight), precision=HIGH) + low(attend_bias)[:, None, None, :]
    split = proj.reshape(3, groups, length, HEADS, HEAD_DIM)
    query = low(rotate(low_back(split[0]), cosine, sine))
    keys = low(rotate(low_back(split[1]), cosine, sine))
    values = low(low_back(split[2]))
    scores = low_back(jnp.einsum('gqhe,gkhe->ghqk', query, keys, precision=HIGH) * HEAD_DIM ** (-0.5))
    scores = jnp.where(allowed[:, None], scores, MASKED)
    top = lax.optimization_barrier(jnp.max(scores, -1, keepdims=True))
    expo = jnp.exp(scores - top)
    probs = low(expo / lax.optimization_barrier(jnp.sum(expo, -1, keepdims=True)))
    context = jnp.einsum('ghqk,gkhe->gqhe', probs, values, precision=HIGH)
    context = low(low_back(context)).reshape(groups, length, D)
    up = low_back(jnp.einsum('gld,df->glf', normed, low(expand_weight), precision=HIGH) + low(expand_bias))
    act = low(gelu_tanh(up))
    branches = jnp.einsum('gld,de->gle', context, low(output_weight), precision=HIGH)
    branches = branches + jnp.einsum('glf,fd->gld', act, low(shrink_weight), precision=HIGH)
    return rows + branches + layer_params[2]

def adamw(weight, grad, first, second, rate, decay, count):
    first_new = BETA_ONE * first + (1.0 - BETA_ONE) * grad
    second_new = BETA_TWO * second + (1.0 - BETA_TWO) * grad * grad
    first_fix = 1.0 - BETA_ONE ** count
    second_fix = 1.0 - BETA_TWO ** count
    update = first_new / first_fix / (jnp.sqrt(second_new / second_fix) + ADAM_EPS)
    return (weight - rate * (update + decay * weight), first_new, second_new)

def reference(inputs, segments, out_grad, layer_params, attend_weight, attend_bias, output_weight, expand_weight, expand_bias, shrink_weight, mean_layer, mean_attend_weight, mean_attend_bias, mean_output_weight, mean_expand_weight, mean_expand_bias, mean_shrink_weight, square_layer, square_attend_weight, square_attend_bias, square_output_weight, square_expand_weight, square_expand_bias, square_shrink_weight):
    count_rows = math.gcd(BATCH, max(1, 2048 // ROW_LEN))
    groups = BATCH // count_rows
    row_data = inputs.astype(jnp.float32).reshape(groups, count_rows, ROW_LEN, D)
    cotangent = out_grad.astype(jnp.float32).reshape(groups, count_rows, ROW_LEN, D)
    seg_rows = segments.reshape(groups, count_rows, ROW_LEN)
    params = (layer_params, attend_weight, attend_bias, output_weight, expand_weight, expand_bias, shrink_weight)
    zero_grads = jax.tree.map(jnp.zeros_like, params)
    places = jnp.arange(ROW_LEN, dtype=jnp.int32)
    causal = places[None, :] <= places[:, None]

    def one_group(total, item):
        rows, back, seg = item
        cosine, sine = rotary_tables(doc_positions(seg))
        allowed = causal[None] & (seg[:, :, None] == seg[:, None, :])
        result, pull = jax.vjp(lambda weights, data: layer(weights, data, cosine, sine, allowed), params, rows)
        grads, grad_rows = pull(back)
        total = jax.tree.map(jnp.add, total, grads)
        return (total, (result.astype(jnp.bfloat16), grad_rows.astype(jnp.bfloat16)))
    grads, (results, input_grads) = lax.scan(one_group, zero_grads, (row_data, cotangent, seg_rows))
    block_output = results.reshape(BATCH, ROW_LEN, D)
    grad_inputs = input_grads.reshape(BATCH, ROW_LEN, D)
    total_sq = sum((jnp.sum(piece * piece) for piece in grads))
    norm_value = jnp.sqrt(total_sq)
    factor = jnp.minimum(1.0, math.sqrt(4 * D * D + 2 * D * FF) / norm_value)
    count = float(STEP)
    firsts = (mean_layer, mean_attend_weight, mean_attend_bias, mean_output_weight, mean_expand_weight, mean_expand_bias, mean_shrink_weight)
    seconds = (square_layer, square_attend_weight, square_attend_bias, square_output_weight, square_expand_weight, square_expand_bias, square_shrink_weight)
    is_matrix = (False, True, False, True, True, False, True)
    weights_new, firsts_new, seconds_new = ([], [], [])
    for weight, grad, first, second, matrix in zip(params, grads, firsts, seconds, is_matrix):
        rate = MATRIX_RATE if matrix else VECTOR_RATE
        decay = DECAY if matrix else 0.0
        weight_new, first_new, second_new = adamw(weight, factor * grad, first, second, rate, decay, count)
        weights_new.append(weight_new)
        firsts_new.append(first_new)
        seconds_new.append(second_new)
    return (block_output, grad_inputs, norm_value.reshape(1), weights_new[0], weights_new[1], weights_new[2], weights_new[3], weights_new[4], weights_new[5], weights_new[6], firsts_new[0], firsts_new[1], firsts_new[2], firsts_new[3], firsts_new[4], firsts_new[5], firsts_new[6], seconds_new[0], seconds_new[1], seconds_new[2], seconds_new[3], seconds_new[4], seconds_new[5], seconds_new[6], weights_new[1].astype(jnp.bfloat16), weights_new[3].astype(jnp.bfloat16), weights_new[4].astype(jnp.bfloat16), weights_new[6].astype(jnp.bfloat16))
```

```python
import math

import jax
import jax.numpy as jnp
from jax import lax
from jax.experimental import pallas as pl
from jax.experimental.pallas import tpu as pltpu
from jax.sharding import PartitionSpec as P

HEAD_DIM = 64
ROT = 32
STEP = 3

EPS_NORM = 1e-05
ROPE_BASE = 10000.0
BETA_ONE = 0.5
BETA_TWO = 0.5
ADAM_EPS = 1e-08
DECAY = 0.1
MATRIX_RATE = 0.03
VECTOR_RATE = 0.3
MASKED = -1e30

AXES = ("dp", "branch")
LOW = jnp.bfloat16
F32 = jnp.float32


def doc_positions(segments):
    length = segments.shape[-1]
    places = jnp.arange(length, dtype=jnp.int32)
    before = jnp.concatenate([segments[..., :1] - 1, segments[..., :-1]], axis=-1)
    starts = jnp.where(segments != before, places, 0)
    starts = lax.cummax(starts, axis=segments.ndim - 1)
    return places - starts


def rotary_lanes(positions):
    half = ROT // 2
    lane = jnp.arange(2 * HEAD_DIM, dtype=jnp.int32) % HEAD_DIM
    freq = ROPE_BASE ** (-((lane % half).astype(F32) * 2.0) / ROT)
    angle = positions.astype(F32)[..., None] * freq
    cosine = jnp.where(lane < ROT, jnp.cos(angle), 1.0)
    sine = jnp.sin(angle)
    up = jnp.where(lane < half, -sine, 0.0)
    down = jnp.where((lane >= half) & (lane < ROT), sine, 0.0)
    return cosine, up, down


def gelu_parts(up):
    inner = 0.7978845608028654 * (up + 0.044715 * up * up * up)
    t = jnp.tanh(inner)
    value = 0.5 * up * (1.0 + t)
    slope = 0.5 * (1.0 + t) + 0.5 * up * (1.0 - t * t) * 0.7978845608028654 * (
        1.0 + 3.0 * 0.044715 * up * up
    )
    return value, slope


def dot(a, b, dims, out=F32):
    return lax.dot_general(a, b, (dims, ((), ())), preferred_element_type=F32).astype(out)


def attention_kernel(q_ref, k_ref, v_ref, d_ref, cos_ref, up_ref, down_ref, segc_ref, segr_ref,
                     ctx_ref, dq_ref, dk_ref, dv_ref, dk_acc, dv_acc):
    length, lanes = q_ref.shape
    half = ROT // 2
    block = length // 2
    scale = HEAD_DIM ** (-0.5)
    cosine, up, down = cos_ref[...], up_ref[...], down_ref[...]

    def rot(x, sign):
        return (x * cosine + sign * (pltpu.roll(x, lanes - half, 1) * up + pltpu.roll(x, half, 1) * down))

    q = rot(q_ref[...], 1.0).astype(LOW)
    k = rot(k_ref[...], 1.0).astype(LOW)
    v = v_ref[...].astype(LOW)
    d = d_ref[...]
    lane = lax.broadcasted_iota(jnp.int32, (length, lanes), 1)
    dk_acc[...] = jnp.zeros_like(dk_acc)
    dv_acc[...] = jnp.zeros_like(dv_acc)
    for i in range(2):
        keys = (i + 1) * block
        rows = slice(i * block, (i + 1) * block)
        place_q = lax.broadcasted_iota(jnp.int32, (block, keys), 0) + i * block
        place_k = lax.broadcasted_iota(jnp.int32, (block, keys), 1)
        allowed = (place_k <= place_q) & (segc_ref[rows, :] == segr_ref[:, :keys])
        ctx = jnp.zeros((block, lanes), F32)
        dq = jnp.zeros((block, lanes), F32)
        for h in range(lanes // HEAD_DIM):
            mine = lane // HEAD_DIM == h
            zero = jnp.zeros((), LOW)
            qm = jnp.where(mine[rows], q[rows], zero)
            dm = jnp.where(mine[rows], d[rows], zero)
            km = jnp.where(mine[:keys], k[:keys], zero)
            vm = jnp.where(mine[:keys], v[:keys], zero)
            s = dot(qm, k[:keys], ((1,), (1,))) * scale
            s = jnp.where(allowed, s, MASKED)
            e = jnp.exp(s - jnp.max(s, -1, keepdims=True))
            p = e * (1.0 / jnp.sum(e, -1, keepdims=True))
            p_low = p.astype(LOW)
            ctx = ctx + dot(p_low, vm, ((1,), (0,)))
            dp = dot(dm, v[:keys], ((1,), (1,)))
            ds = (p * (dp - jnp.sum(p * dp, -1, keepdims=True))).astype(LOW)
            dq = dq + dot(ds, km, ((1,), (0,)))
            dk_acc[:keys, :] += dot(ds, qm, ((0,), (0,)))
            dv_acc[:keys, :] += dot(p_low, dm, ((0,), (0,)))
        ctx_ref[rows, :] = ctx.astype(LOW)
        dq = dq * scale
        dq_ref[rows, :] = (
            dq * cosine[rows]
            - (pltpu.roll(dq, lanes - half, 1) * up[rows] + pltpu.roll(dq, half, 1) * down[rows])
        ).astype(LOW)
    dk_ref[...] = rot(dk_acc[...] * scale, -1.0).astype(LOW)
    dv_ref[...] = dv_acc[...].astype(LOW)


def attention(proj, d_context, segments):
    rows, length = segments.shape
    width = d_context.shape[1]
    pair = 2 * HEAD_DIM
    pairs = width // pair
    cosine, up, down = rotary_lanes(doc_positions(segments).reshape(rows * length))
    part = lambda c: pl.BlockSpec((length, pair), lambda r, h: (r, c * pairs + h))
    table = pl.BlockSpec((length, pair), lambda r, h: (r, 0))
    out = jax.ShapeDtypeStruct((rows * length, width), LOW)
    return pl.pallas_call(
        attention_kernel,
        grid=(rows, pairs),
        in_specs=[
            part(0), part(1), part(2), part(0), table, table, table,
            pl.BlockSpec((length, 1), lambda r, h: (r, 0)),
            pl.BlockSpec((None, 1, length), lambda r, h: (r, 0, 0)),
        ],
        out_specs=[part(0)] * 4,
        out_shape=[out] * 4,
        scratch_shapes=[pltpu.VMEM((length, pair), F32)] * 2,
        cost_estimate=pl.CostEstimate(
            flops=14 * rows * length * length * width,
            bytes_accessed=rows * length * width * 24,
            transcendentals=rows * length * length * width // HEAD_DIM,
        ),
    )(proj, proj, proj, d_context, cosine, up, down,
      segments.reshape(rows * length, 1), segments.reshape(rows, 1, length))


class Place:
    def __init__(self, nd, nb):
        self.nz, self.nb = nd // 2, nb
        dp, branch = lax.axis_index("dp"), lax.axis_index("branch")
        self.dp, self.branch = dp, branch
        self.z, self.x = dp // 2, dp % 2
        self.y, self.c = branch // 2, branch % 2

    def send(self, value, to):
        pairs = []
        for z in range(self.nz):
            for x in range(2):
                for b in range(self.nb):
                    t = to(z, x, b // 2, b % 2)
                    if t is not None:
                        pairs.append(((2 * z + x) * self.nb + b, (2 * t[0] + t[1]) * self.nb + 2 * t[2] + t[3]))
        return lax.ppermute(value, AXES, perm=pairs)

    def swap_x(self, v):
        return self.send(v, lambda z, x, y, c: (z, 1 - x, y, c))

    def swap_c(self, v):
        return self.send(v, lambda z, x, y, c: (z, x, y, 1 - c))

    def swap_first(self, v):
        return self.send(v, lambda z, x, y, c: (z, 1 - x, y, c) if c == 0 else (z, x, 1 - y, c))

    def swap_second(self, v):
        return self.send(v, lambda z, x, y, c: (z, x, 1 - y, c) if c == 0 else (z, 1 - x, y, c))

    def along_z(self, v, hops):
        return self.send(v, lambda z, x, y, c: (hops[z], x, y, c) if z in hops else None)


def gather_tokens(at, own):
    rows, block, d = own.shape
    first = at.swap_first(own)
    second = at.swap_second(own)
    third = at.swap_second(first)
    pieces = [own, first, second, third]
    full = jnp.zeros((2, rows, at.nb, block, d), own.dtype)
    c0 = at.c == 0
    flips = [(0, 0), (jnp.where(c0, 1, 0), jnp.where(c0, 0, 1)), (jnp.where(c0, 0, 1), jnp.where(c0, 1, 0)), (1, 1)]
    for piece, (fx, fy) in zip(pieces, flips):
        for other in (0, 1):
            here = at.swap_c(piece) if other else piece
            if other:
                gx, gy = (fy, fx)
            else:
                gx, gy = (fx, fy)
            spot = (at.x + gx) % 2, 2 * ((at.y + gy) % 2) + (at.c + other) % 2
            full = lax.dynamic_update_slice(
                full, here[None, :, None], (spot[0], 0, spot[1], 0, 0))
    return full


def scatter_tokens(at, part):
    _, rows, nb, block, d = part.shape
    part = part.reshape(2, rows, 2, 2, block, d)
    pick = lambda v, i, axis: lax.dynamic_index_in_dim(v, i, axis, keepdims=False)
    got = at.swap_c(pick(part, 1 - at.c, 3))
    p = pick(part, at.c, 3).astype(F32) + got.astype(F32)
    c0 = at.c == 0
    by_y = lambda v, i: pick(v, i, 2)
    by_x = lambda v, i: jnp.moveaxis(pick(v, i, 0), 1, 0)
    got = at.swap_second(jnp.where(c0, by_y(p, 1 - at.y), by_x(p, 1 - at.x)).astype(LOW))
    q = jnp.where(c0, by_y(p, at.y), by_x(p, at.x)) + got.astype(F32)
    i = jnp.where(c0, at.x, at.y)
    got = at.swap_first(pick(q, 1 - i, 0).astype(LOW))
    return pick(q, i, 0) + got.astype(F32)


def gather_z(at, chunk):
    if at.nz == 4:
        odd = at.z % 2 == 1
        got = at.along_z(chunk, {0: 1, 1: 0, 2: 3, 3: 2})
        two = jnp.where(odd, jnp.concatenate([got, chunk]), jnp.concatenate([chunk, got]))
        near = at.along_z(two, {1: 2, 2: 1})
        far = at.along_z(near, {1: 0, 2: 3})
        rest = jnp.where((at.z == 1) | (at.z == 2), near, far)
        return jnp.where(at.z < 2, jnp.concatenate([two, rest]), jnp.concatenate([rest, two]))
    n, cols = chunk.shape
    full = jnp.zeros((at.nz * n, cols), chunk.dtype)
    ring = {z: (z + 1) % at.nz for z in range(at.nz)}
    for step in range(at.nz):
        full = lax.dynamic_update_slice(full, chunk, (((at.z - step) % at.nz) * n, 0))
        if step < at.nz - 1:
            chunk = at.along_z(chunk, ring)
    return full


def scatter_z(at, part):
    n = part.shape[0] // at.nz
    part = part.reshape(at.nz, n, part.shape[1])
    pick = lambda v, i: lax.dynamic_index_in_dim(v, i, 0, keepdims=False)
    if at.nz == 4:
        half = at.z // 2
        mine = lax.dynamic_slice_in_dim(part, 2 * half, 2, 0)
        away = lax.dynamic_slice_in_dim(part, 2 - 2 * half, 2, 0)
        got = at.along_z(away, {0: 1, 3: 2})
        got = at.along_z((away.astype(F32) + got.astype(F32)).astype(LOW), {1: 2, 2: 1})
        total = mine.astype(F32) + got.astype(F32)
        got = at.along_z(pick(total, 1 - at.z % 2).astype(LOW), {0: 1, 1: 0, 2: 3, 3: 2})
        return pick(total, at.z % 2) + got.astype(F32)
    ring = {z: (z + 1) % at.nz for z in range(at.nz)}
    total = pick(part, (at.z - 1) % at.nz).astype(F32)
    for step in range(1, at.nz):
        got = at.along_z(total.astype(LOW), ring)
        total = pick(part, (at.z - 1 - step) % at.nz).astype(F32) + got.astype(F32)
    return total


def adamw(weight, grad, first, second, rate, decay, count):
    first_new = BETA_ONE * first + (1.0 - BETA_ONE) * grad
    second_new = BETA_TWO * second + (1.0 - BETA_TWO) * grad * grad
    first_fix = 1.0 - BETA_ONE**count
    second_fix = 1.0 - BETA_TWO**count
    update = first_new / first_fix / (jnp.sqrt(second_new / second_fix) + ADAM_EPS)
    return (weight - rate * (update + decay * weight), first_new, second_new)


def on_device(
    nd,
    nb,
    inputs,
    segments,
    out_grad,
    layer_params,
    attend_weight,
    attend_bias,
    output_weight,
    expand_weight,
    expand_bias,
    shrink_weight,
    mean_layer,
    mean_attend_weight,
    mean_attend_bias,
    mean_output_weight,
    mean_expand_weight,
    mean_expand_bias,
    mean_shrink_weight,
    square_layer,
    square_attend_weight,
    square_attend_bias,
    square_output_weight,
    square_expand_weight,
    square_expand_bias,
    square_shrink_weight,
):
    at = Place(nd, nb)
    x0 = at.x == 0
    rows, block, d = inputs.shape
    length = segments.shape[1]
    tokens = 2 * rows * length
    heads2 = attend_weight.shape[2] // 2
    hidden2 = expand_weight.shape[1] // 2
    gain, shift, out_bias = layer_params[0], layer_params[1], layer_params[2]

    data = inputs.astype(F32)
    center = data - jnp.mean(data, -1, keepdims=True)
    inverse = lax.rsqrt(jnp.mean(center * center, -1, keepdims=True) + EPS_NORM)
    normal = center * inverse
    normed = (normal * gain + shift).astype(LOW)

    def halves(h):
        cols = lambda w: lax.dynamic_slice_in_dim(w, h * heads2, heads2, w.ndim - 1)
        att = attend_weight.astype(LOW)
        attend = jnp.concatenate(
            [cols(att[0]), cols(att[1]), cols(att[2]),
             lax.dynamic_slice_in_dim(output_weight.astype(LOW), h * heads2, heads2, 0).T], 1)
        expand = lax.dynamic_slice_in_dim(expand_weight.astype(LOW), h * hidden2, hidden2, 1)
        shrink = lax.dynamic_slice_in_dim(shrink_weight.astype(LOW), h * hidden2, hidden2, 0).T
        return attend, expand, shrink

    whole = []
    for mine, theirs in zip(halves(at.x), halves(1 - at.x)):
        got = at.swap_x(theirs)
        chunk = jnp.where(x0, jnp.concatenate([mine, got]), jnp.concatenate([got, mine]))
        whole.append(gather_z(at, chunk))
    attend, expand, shrink = whole
    biases = jnp.concatenate([attend_bias.reshape(-1), expand_bias]).astype(LOW)
    biases = lax.all_gather(biases, "dp", axis=0)
    n_att = attend_bias.shape[1]
    bias_att = jnp.moveaxis(biases[:, : 3 * n_att].reshape(nd, 3, n_att), 0, 1).reshape(3, -1)
    bias_att = lax.dynamic_slice_in_dim(bias_att, at.x * heads2, heads2, 1).astype(F32)
    bias_exp = lax.dynamic_slice_in_dim(
        biases[:, 3 * n_att:].reshape(-1), at.x * hidden2, hidden2, 0).astype(F32)

    tok = gather_tokens(at, normed).reshape(tokens, d)
    dy = gather_tokens(at, out_grad).reshape(tokens, d)
    got = at.swap_x(segments)
    segs = jnp.where(x0, jnp.concatenate([segments, got]), jnp.concatenate([got, segments]))

    att_w, wo_t = attend[:, : 3 * heads2], attend[:, 3 * heads2:]
    proj = dot(tok, att_w, ((1,), (0,))) + bias_att.reshape(-1)
    d_context = dot(dy, wo_t, ((1,), (0,)), LOW)
    context, d_query, d_key, d_value = attention(proj, d_context, segs)
    d_proj = jnp.concatenate([d_query, d_key, d_value], 1)

    up = dot(tok, expand, ((1,), (0,))) + bias_exp
    act, slope = gelu_parts(up)
    act = act.astype(LOW)
    d_up = (dot(dy, shrink, ((1,), (0,))) * slope).astype(LOW)

    grad_attend = jnp.concatenate(
        [dot(tok, d_proj, ((0,), (0,)), LOW), dot(dy, context, ((0,), (0,)), LOW)], 1)
    grad_shrink = dot(dy, act, ((0,), (0,)), LOW)
    grad_expand = dot(tok, d_up, ((0,), (0,)), LOW)

    def owned(part):
        total = scatter_z(at, part)
        total = total.reshape(2, total.shape[0] // 2, total.shape[1])
        pick = lambda i: lax.dynamic_index_in_dim(total, i, 0, keepdims=False)
        mine = pick(at.x)
        got = at.swap_x(pick(1 - at.x).astype(LOW)).astype(F32)
        return jnp.where(x0, mine, got), jnp.where(x0, got, mine)

    lo_a, hi_a = owned(grad_attend)
    lo_s, hi_s = owned(grad_shrink)
    lo_e, hi_e = owned(grad_expand)
    join = lambda i: jnp.concatenate(
        [lo_a[:, i * heads2:(i + 1) * heads2], hi_a[:, i * heads2:(i + 1) * heads2]], 1)
    g_attend = jnp.stack([join(0), join(1), join(2)])
    g_output = join(3).T
    g_expand = jnp.concatenate([lo_e, hi_e], 1)
    g_shrink = jnp.concatenate([lo_s, hi_s], 1).T

    partial = dot(act, shrink, ((1,), (1,))) + dot(context, wo_t, ((1,), (1,)))
    partial = partial.astype(LOW).reshape(2, rows, nb, block, d)
    summed = scatter_tokens(at, partial)
    result = (data + summed + out_bias).astype(LOW)

    partial = dot(d_up, expand, ((1,), (1,))) + dot(d_proj, att_w, ((1,), (1,)))
    partial = partial.astype(LOW).reshape(2, rows, nb, block, d)
    d_normed = scatter_tokens(at, partial)
    grad_gain = jnp.sum(d_normed * normal, (0, 1))
    grad_shift = jnp.sum(d_normed, (0, 1))
    d_normal = d_normed * gain
    d_rows = inverse * (
        d_normal
        - jnp.mean(d_normal, -1, keepdims=True)
        - normal * jnp.mean(d_normal * normal, -1, keepdims=True)
    )
    back = out_grad.astype(F32)
    d_rows = (d_rows + back).astype(LOW)

    sum_att = jnp.sum(d_proj.astype(F32), 0).reshape(3, heads2)
    sum_exp = jnp.sum(d_up.astype(F32), 0)
    spread_att = lax.dynamic_update_slice(jnp.zeros((3, 2 * heads2), F32), sum_att, (0, at.x * heads2))
    spread_exp = lax.dynamic_update_slice(jnp.zeros((2 * hidden2,), F32), sum_exp, (at.x * hidden2,))
    spread = lax.psum(jnp.concatenate([spread_att.reshape(-1), spread_exp]), "dp")
    n_exp = expand_bias.shape[0]
    g_bias_att = lax.dynamic_slice_in_dim(
        spread[: 6 * heads2].reshape(3, 2 * heads2), at.dp * n_att, n_att, 1)
    g_bias_exp = lax.dynamic_slice_in_dim(spread[6 * heads2:], at.dp * n_exp, n_exp, 0)

    small = jnp.stack([grad_gain, grad_shift, jnp.sum(back, (0, 1))])
    pieces = (lo_a, hi_a, lo_s, hi_s, lo_e, hi_e, g_bias_att, g_bias_exp)
    squares = sum(jnp.sum(piece * piece) for piece in pieces)
    g_small, squares = lax.psum((small, squares), AXES)
    norm_value = jnp.sqrt(squares + jnp.sum(g_small * g_small))
    size = 4 * d * d + 2 * d * 2 * hidden2 * nb
    factor = jnp.minimum(1.0, math.sqrt(size) / norm_value)
    count = float(STEP)
    params = (layer_params, attend_weight, attend_bias, output_weight, expand_weight, expand_bias, shrink_weight)
    grads = (g_small, g_attend, g_bias_att, g_output, g_expand, g_bias_exp, g_shrink)
    firsts = (mean_layer, mean_attend_weight, mean_attend_bias, mean_output_weight, mean_expand_weight,
              mean_expand_bias, mean_shrink_weight)
    seconds = (square_layer, square_attend_weight, square_attend_bias, square_output_weight,
               square_expand_weight, square_expand_bias, square_shrink_weight)
    is_matrix = (False, True, False, True, True, False, True)
    weights_new, firsts_new, seconds_new = ([], [], [])
    for weight, grad, first, second, matrix in zip(params, grads, firsts, seconds, is_matrix):
        rate = MATRIX_RATE if matrix else VECTOR_RATE
        decay = DECAY if matrix else 0.0
        new = adamw(weight, factor * grad, first, second, rate, decay, count)
        weights_new.append(new[0])
        firsts_new.append(new[1])
        seconds_new.append(new[2])
    return (
        result,
        d_rows,
        norm_value.reshape(1),
        *weights_new,
        *firsts_new,
        *seconds_new,
        weights_new[1].astype(LOW),
        weights_new[3].astype(LOW),
        weights_new[4].astype(LOW),
        weights_new[6].astype(LOW),
    )


def solution(mesh):
    nd, nb = mesh.shape["dp"], mesh.shape["branch"]
    state = (
        P(),
        P(None, "dp", "branch"),
        P(None, ("branch", "dp")),
        P("branch", "dp"),
        P("dp", "branch"),
        P(("branch", "dp")),
        P("branch", "dp"),
    )
    rows = P("dp", "branch", None)
    return jax.shard_map(
        lambda *args: on_device(nd, nb, *args),
        mesh=mesh,
        in_specs=(rows, P("dp", None), rows) + state * 3,
        out_specs=(rows, rows, P()) + state * 3 + (state[1], state[3], state[4], state[6]),
        check_vma=False,
    )
```

```python
import functools
import math

import jax
import jax.numpy as jnp
from jax import lax
from jax.experimental import pallas as pl
from jax.experimental.pallas import tpu as pltpu
from jax.sharding import PartitionSpec as P

HEAD_DIM = 64
ROT = 32
STEP = 3

EPS_NORM = 1e-05
ROPE_BASE = 10000.0
BETA_ONE = 0.5
BETA_TWO = 0.5
ADAM_EPS = 1e-08
DECAY = 0.1
MATRIX_RATE = 0.03
VECTOR_RATE = 0.3
MASKED = -1e30

AXES = ("dp", "branch")
LOW = jnp.bfloat16
F32 = jnp.float32


def doc_positions(segments):
    length = segments.shape[-1]
    places = jnp.arange(length, dtype=jnp.int32)
    before = jnp.concatenate([segments[..., :1] - 1, segments[..., :-1]], axis=-1)
    starts = jnp.where(segments != before, places, 0)
    starts = lax.cummax(starts, axis=segments.ndim - 1)
    return places - starts


def rotary_lanes(positions):
    half = ROT // 2
    lane = jnp.arange(2 * HEAD_DIM, dtype=jnp.int32) % HEAD_DIM
    freq = ROPE_BASE ** (-((lane % half).astype(F32) * 2.0) / ROT)
    angle = positions.astype(F32)[..., None] * freq
    cosine = jnp.where(lane < ROT, jnp.cos(angle), 1.0)
    sine = jnp.sin(angle)
    up = jnp.where(lane < half, -sine, 0.0)
    down = jnp.where((lane >= half) & (lane < ROT), sine, 0.0)
    return cosine, up, down


def gelu_parts(up):
    inner = 0.7978845608028654 * (up + 0.044715 * up * up * up)
    t = jnp.tanh(inner)
    value = 0.5 * up * (1.0 + t)
    slope = 0.5 * (1.0 + t) + 0.5 * up * (1.0 - t * t) * 0.7978845608028654 * (
        1.0 + 3.0 * 0.044715 * up * up
    )
    return value, slope


def dot(a, b, dims, out=F32):
    return lax.dot_general(a, b, (dims, ((), ())), preferred_element_type=F32).astype(out)


def attention_kernel(q_ref, k_ref, v_ref, d_ref, cos_ref, up_ref, down_ref, segc_ref, segr_ref,
                     ctx_ref, dq_ref, dk_ref, dv_ref, dk_acc, dv_acc):
    length, lanes = q_ref.shape
    half = ROT // 2
    block = length // 2
    scale = HEAD_DIM ** (-0.5)
    cosine, up, down = cos_ref[...], up_ref[...], down_ref[...]

    def rot(x, sign):
        return (x * cosine + sign * (pltpu.roll(x, lanes - half, 1) * up + pltpu.roll(x, half, 1) * down))

    q = rot(q_ref[...], 1.0).astype(LOW)
    k = rot(k_ref[...], 1.0).astype(LOW)
    v = v_ref[...].astype(LOW)
    d = d_ref[...]
    lane = lax.broadcasted_iota(jnp.int32, (length, lanes), 1)
    dk_acc[...] = jnp.zeros_like(dk_acc)
    dv_acc[...] = jnp.zeros_like(dv_acc)
    for i in range(2):
        keys = (i + 1) * block
        rows = slice(i * block, (i + 1) * block)
        place_q = lax.broadcasted_iota(jnp.int32, (block, keys), 0) + i * block
        place_k = lax.broadcasted_iota(jnp.int32, (block, keys), 1)
        allowed = (place_k <= place_q) & (segc_ref[rows, :] == segr_ref[:, :keys])
        ctx = jnp.zeros((block, lanes), F32)
        dq = jnp.zeros((block, lanes), F32)
        for h in range(lanes // HEAD_DIM):
            mine = lane // HEAD_DIM == h
            zero = jnp.zeros((), LOW)
            qm = jnp.where(mine[rows], q[rows], zero)
            dm = jnp.where(mine[rows], d[rows], zero)
            km = jnp.where(mine[:keys], k[:keys], zero)
            vm = jnp.where(mine[:keys], v[:keys], zero)
            s = dot(qm, k[:keys], ((1,), (1,))) * scale
            s = jnp.where(allowed, s, MASKED)
            e = jnp.exp(s - jnp.max(s, -1, keepdims=True))
            p = e * (1.0 / jnp.sum(e, -1, keepdims=True))
            p_low = p.astype(LOW)
            ctx = ctx + dot(p_low, vm, ((1,), (0,)))
            dp = dot(dm, v[:keys], ((1,), (1,)))
            ds = (p * (dp - jnp.sum(p * dp, -1, keepdims=True))).astype(LOW)
            dq = dq + dot(ds, km, ((1,), (0,)))
            dk_acc[:keys, :] += dot(ds, qm, ((0,), (0,)))
            dv_acc[:keys, :] += dot(p_low, dm, ((0,), (0,)))
        ctx_ref[rows, :] = ctx.astype(LOW)
        dq = dq * scale
        dq_ref[rows, :] = (
            dq * cosine[rows]
            - (pltpu.roll(dq, lanes - half, 1) * up[rows] + pltpu.roll(dq, half, 1) * down[rows])
        ).astype(LOW)
    dk_ref[...] = rot(dk_acc[...] * scale, -1.0).astype(LOW)
    dv_ref[...] = dv_acc[...].astype(LOW)


def attention(proj, d_context, segments):
    rows, length = segments.shape
    width = d_context.shape[1]
    pair = 2 * HEAD_DIM
    pairs = width // pair
    cosine, up, down = rotary_lanes(doc_positions(segments).reshape(rows * length))
    part = lambda c: pl.BlockSpec((length, pair), lambda r, h: (r, c * pairs + h))
    table = pl.BlockSpec((length, pair), lambda r, h: (r, 0))
    out = jax.ShapeDtypeStruct((rows * length, width), LOW)
    return pl.pallas_call(
        attention_kernel,
        grid=(rows, pairs),
        in_specs=[
            part(0), part(1), part(2), part(0), table, table, table,
            pl.BlockSpec((length, 1), lambda r, h: (r, 0)),
            pl.BlockSpec((None, 1, length), lambda r, h: (r, 0, 0)),
        ],
        out_specs=[part(0)] * 4,
        out_shape=[out] * 4,
        scratch_shapes=[pltpu.VMEM((length, pair), F32)] * 2,
        cost_estimate=pl.CostEstimate(
            flops=14 * rows * length * length * width,
            bytes_accessed=rows * length * width * 24,
            transcendentals=rows * length * length * width // HEAD_DIM,
        ),
    )(proj, proj, proj, d_context, cosine, up, down,
      segments.reshape(rows * length, 1), segments.reshape(rows, 1, length))


MESH = pl.DeviceIdType.MESH


def here(nz, nb):
    dp, branch = lax.axis_index("dp"), lax.axis_index("branch")
    return dp // 2, dp % 2, branch // 2, branch % 2


def head_kernel(nz, nb, nrm, dyo, pack, bias, seg, tok, dy, wts, biases, segs,
                local, t_send, t_recv, d_send, d_recv, x_send, x_recv, z_send, z_recv, s_send, s_recv):
    z, x, y, c = here(nz, nb)
    ident = lambda z, x, y, c: (2 * z + x, 2 * y + c)
    first = (z, (x + 1 - c) % 2, (y + c) % 2, c)
    second = (z, (x + c) % 2, (y + 1 - c) % 2, c)
    sib = (z, x, y, 1 - c)
    across = (z, 1 - x, y, c)

    barrier = pltpu.get_barrier_semaphore()
    for t in (across, (z, x, 1 - y, c), sib):
        pl.semaphore_signal(barrier, inc=1, device_id=ident(*t), device_id_type=MESH)

    @pl.when(z > 0)
    def _():
        pl.semaphore_signal(barrier, inc=1, device_id=ident(z - 1, x, y, c), device_id_type=MESH)

    @pl.when(z < nz - 1)
    def _():
        pl.semaphore_signal(barrier, inc=1, device_id=ident(z + 1, x, y, c), device_id_type=MESH)

    pl.semaphore_wait(barrier, 3 + jnp.minimum(z, 1) + jnp.minimum(nz - 1 - z, 1))

    def remote(src, dst, send, recv, to):
        return pltpu.make_async_remote_copy(
            src_ref=src, dst_ref=dst, send_sem=send, recv_sem=recv, device_id=ident(*to), device_id_type=MESH)

    class Tokens:
        def __init__(self, src, out, send, recv):
            self.src, self.out, self.send, self.recv = src, out, send, recv

        def spot(self, dev):
            return self.out.at[dev[1], :, 2 * dev[2] + dev[3]]

        def copy(self, k):
            me = (z, x, y, c)
            opp = (z, 1 - x, 1 - y, c)
            where, to = [(me, sib), (me, first), (me, second), (first, second), (first, sib), (second, sib), (opp, sib)][k]
            src = self.src if k < 3 else self.spot(where)
            return remote(src, self.spot(where), self.send.at[k], self.recv.at[k], to)

    nt, dt = Tokens(nrm, tok, t_send, t_recv), Tokens(dyo, dy, d_send, d_recv)

    def zcopy(k, step, right):
        origin = z - (step - 1) if right else z + (step - 1)
        col = x if k == 0 else 1 - x
        src = wts.at[origin, col]
        if step == 1 and k == 0:
            src = pack.at[x]
        to = (z + 1 if right else z - 1, x, y, c)
        sem = (k, step - 1, 0 if right else 1)
        return remote(src, wts.at[origin, col], z_send.at[sem], z_recv.at[sem], to)

    def zsends(step, right):
        if right:
            return (z - (step - 1) >= 0) & (z + 1 <= nz - 1)
        return (z + (step - 1) <= nz - 1) & (z - 1 >= 0)

    def zgets(step, right):
        return (z - step >= 0) if right else (z + step <= nz - 1)

    def zstart(k, step):
        for right in (True, False):
            @pl.when(zsends(step, right))
            def _():
                zcopy(k, step, right).start()

    def zarrive(k, step):
        for right in (True, False):
            @pl.when(zgets(step, right))
            def _():
                zcopy(k, step, right).wait_recv()

    swap = remote(pack.at[1 - x], wts.at[z, x], x_send.at[0], x_recv.at[0], across)
    own = [
        pltpu.make_async_copy(nrm, nt.spot((z, x, y, c)), local.at[0]),
        pltpu.make_async_copy(dyo, dt.spot((z, x, y, c)), local.at[1]),
        pltpu.make_async_copy(pack.at[x], wts.at[z, x], local.at[2]),
        pltpu.make_async_copy(bias, biases.at[2 * z + x], local.at[3]),
        pltpu.make_async_copy(seg, segs.at[x], local.at[4]),
    ]
    bias_x = remote(bias, biases.at[2 * z + x], s_send.at[0], s_recv.at[0], across)
    seg_x = remote(seg, segs.at[x], x_send.at[1], x_recv.at[1], across)

    def bcopy(step, right, k):
        origin = z - (step - 1) if right else z + (step - 1)
        row = 2 * origin + (x if k == 0 else 1 - x)
        sem = 1 + 4 * (step - 1) + 2 * k + (0 if right else 1)
        to = (z + 1 if right else z - 1, x, y, c)
        return remote(biases.at[row], biases.at[row], s_send.at[sem], s_recv.at[sem], to)

    swap.start()
    zstart(0, 1)
    nt.copy(1).start()
    nt.copy(2).start()
    nt.copy(0).start()
    for copy in own:
        copy.start()
    bias_x.start()
    seg_x.start()
    own[3].wait()
    bias_x.wait_recv()
    swap.wait_recv()
    zstart(1, 1)
    for step in range(1, nz):
        for k in (0, 1):
            for right in (True, False):
                @pl.when(zsends(step, right))
                def _():
                    bcopy(step, right, k).start()
        if step == 1:
            dt.copy(0).start()
            nt.copy(1).wait_recv()
            nt.copy(3).start()
            nt.copy(4).start()
            dt.copy(1).start()
            dt.copy(2).start()
        for k in (0, 1):
            zarrive(k, step)
            if step < nz - 1:
                zstart(k, step + 1)
        for k in (0, 1):
            for right in (True, False):
                @pl.when(zgets(step, right))
                def _():
                    bcopy(step, right, k).wait_recv()
        if step == 1:
            nt.copy(2).wait_recv()
            nt.copy(5).start()
            dt.copy(1).wait_recv()
            dt.copy(3).start()
            dt.copy(4).start()
            nt.copy(3).wait_recv()
            nt.copy(6).start()
        if step == min(2, nz - 1):
            dt.copy(2).wait_recv()
            dt.copy(5).start()
            dt.copy(3).wait_recv()
            dt.copy(6).start()
    for t in (nt, dt):
        for k in (0, 4, 5, 6):
            t.copy(k).wait_recv()
        for k in range(7):
            t.copy(k).wait_send()
    for step in range(1, nz):
        for k in (0, 1):
            for right in (True, False):
                @pl.when(zsends(step, right))
                def _():
                    zcopy(k, step, right).wait_send()
                    bcopy(step, right, k).wait_send()
    swap.wait_send()
    bias_x.wait_send()
    seg_x.wait()
    for i, copy in enumerate(own):
        if i != 3:
            copy.wait()


def head(nz, nb, nrm, dyo, pack, bias, seg):
    rows, block, d = nrm.shape
    anywhere = pl.BlockSpec(memory_space=pl.ANY)
    dma = pltpu.SemaphoreType.DMA
    full = jax.ShapeDtypeStruct((2, rows, nb, block, d), nrm.dtype)
    return pl.pallas_call(
        functools.partial(head_kernel, nz, nb),
        in_specs=[anywhere] * 5,
        out_specs=[anywhere] * 5,
        out_shape=[
            full, full,
            jax.ShapeDtypeStruct((nz,) + pack.shape, pack.dtype),
            jax.ShapeDtypeStruct((2 * nz,) + bias.shape, bias.dtype),
            jax.ShapeDtypeStruct((2,) + seg.shape, seg.dtype),
        ],
        scratch_shapes=[
            dma((5,)), dma((7,)), dma((7,)), dma((7,)), dma((7,)), dma((2,)), dma((2,)),
            dma((2, nz - 1, 2)), dma((2, nz - 1, 2)), dma((4 * nz,)), dma((4 * nz,)),
        ],
        compiler_params=pltpu.CompilerParams(collective_id=0, has_side_effects=True),
        name="head",
    )(nrm, dyo, pack, bias, seg)


def sums_kernel(nz, nb, n_small, n_bias, mine, out, other, acc, slots, send, recv):
    z, x, y, c = here(nz, nb)
    ident = lambda z, x, y, c: (2 * z + x, 2 * y + c)
    rounds = []
    step = 1
    while step < nz:
        far = (z // step) % 2
        rounds.append(((z + step - 2 * step * far, x, y, c), "z"))
        step *= 2
    rounds += [((z, 1 - x, y, c), "x"), ((z, x, 1 - y, c), "y"), ((z, x, y, 1 - c), "c")]
    barrier = pltpu.get_barrier_semaphore()
    for to, _ in rounds:
        pl.semaphore_signal(barrier, inc=1, device_id=ident(*to), device_id_type=MESH)
    pl.semaphore_wait(barrier, len(rounds))
    acc[...] = mine[...]
    biases = slice(n_small, n_small + n_bias)
    done_z = False
    copies = []
    for r, (to, kind) in enumerate(rounds):
        if kind != "z" and not done_z:
            done_z = True
            total = acc[biases, :]
            acc[n_small + n_bias:, :] += jnp.sum(total * total) * (
                (lax.broadcasted_iota(jnp.int32, (8, 128), 0) == 0)
                & (lax.broadcasted_iota(jnp.int32, (8, 128), 1) == 0)
            ).astype(F32)
            out[biases, :] = total
        slots[0, r] = acc[...]
        copy = pltpu.make_async_remote_copy(
            src_ref=slots.at[0, r], dst_ref=slots.at[1, r], send_sem=send.at[r], recv_sem=recv.at[r],
            device_id=ident(*to), device_id_type=MESH)
        copy.start()
        copies.append(copy)
        copy.wait_recv()
        acc[...] += slots[1, r]
        if kind == "x":
            other[...] = slots[1, r, biases, :]
    out[:n_small, :] = acc[:n_small, :]
    out[n_small + n_bias:, :] = acc[n_small + n_bias:, :]
    for copy in copies:
        copy.wait_send()


def sums(nz, nb, small, bias, squares):
    pad = -bias.size % 1024
    rows = [small.reshape(-1, 128), jnp.pad(bias, (0, pad)).reshape(-1, 128), jnp.pad(squares.reshape(1, 1), ((0, 7), (0, 127)))]
    n_small, n_bias = rows[0].shape[0], rows[1].shape[0]
    n = n_small + n_bias + 8
    n_rounds = int(math.log2(nz)) + 3
    vmem = pl.BlockSpec(memory_space=pltpu.VMEM)
    dma = pltpu.SemaphoreType.DMA
    out, other = pl.pallas_call(
        functools.partial(sums_kernel, nz, nb, n_small, n_bias),
        in_specs=[vmem],
        out_specs=[vmem, vmem],
        out_shape=[jax.ShapeDtypeStruct((n, 128), F32), jax.ShapeDtypeStruct((n_bias, 128), F32)],
        scratch_shapes=[
            pltpu.VMEM((n, 128), F32), pltpu.VMEM((2, n_rounds, n, 128), F32), dma((n_rounds,)), dma((n_rounds,))],
        compiler_params=pltpu.CompilerParams(collective_id=1, has_side_effects=True),
        name="sums",
    )(jnp.concatenate(rows))
    flat = lambda v: v.reshape(-1)[: bias.size]
    return (out[:n_small].reshape(small.shape), flat(out[n_small:n_small + n_bias]), flat(other),
            out[n_small + n_bias, 0])


class Place:
    def __init__(self, nd, nb):
        self.nz, self.nb = nd // 2, nb
        dp, branch = lax.axis_index("dp"), lax.axis_index("branch")
        self.dp, self.branch = dp, branch
        self.z, self.x = dp // 2, dp % 2
        self.y, self.c = branch // 2, branch % 2

    def send(self, value, to):
        pairs = []
        for z in range(self.nz):
            for x in range(2):
                for b in range(self.nb):
                    t = to(z, x, b // 2, b % 2)
                    if t is not None:
                        pairs.append(((2 * z + x) * self.nb + b, (2 * t[0] + t[1]) * self.nb + 2 * t[2] + t[3]))
        return lax.ppermute(value, AXES, perm=pairs)

    def swap_x(self, v):
        return self.send(v, lambda z, x, y, c: (z, 1 - x, y, c))

    def swap_c(self, v):
        return self.send(v, lambda z, x, y, c: (z, x, y, 1 - c))

    def swap_first(self, v):
        return self.send(v, lambda z, x, y, c: (z, 1 - x, y, c) if c == 0 else (z, x, 1 - y, c))

    def swap_second(self, v):
        return self.send(v, lambda z, x, y, c: (z, x, 1 - y, c) if c == 0 else (z, 1 - x, y, c))

    def along_z(self, v, hops):
        return self.send(v, lambda z, x, y, c: (hops[z], x, y, c) if z in hops else None)


def scatter_tokens(at, part):
    _, rows, nb, block, d = part.shape
    part = part.reshape(2, rows, 2, 2, block, d)
    pick = lambda v, i, axis: lax.dynamic_index_in_dim(v, i, axis, keepdims=False)
    got = at.swap_c(pick(part, 1 - at.c, 3))
    p = pick(part, at.c, 3).astype(F32) + got.astype(F32)
    c0 = at.c == 0
    by_y = lambda v, i: pick(v, i, 2)
    by_x = lambda v, i: jnp.moveaxis(pick(v, i, 0), 1, 0)
    got = at.swap_second(jnp.where(c0, by_y(p, 1 - at.y), by_x(p, 1 - at.x)).astype(LOW))
    q = jnp.where(c0, by_y(p, at.y), by_x(p, at.x)) + got.astype(F32)
    i = jnp.where(c0, at.x, at.y)
    got = at.swap_first(pick(q, 1 - i, 0).astype(LOW))
    return pick(q, i, 0) + got.astype(F32)


def over_z(at):
    return [[2 * z + x for z in range(at.nz)] for x in range(2)]


def gather_z(at, chunk):
    return lax.all_gather(chunk, "dp", axis=0, tiled=True, axis_index_groups=over_z(at))


def scatter_z(at, part):
    return lax.psum_scatter(part, "dp", scatter_dimension=0, tiled=True, axis_index_groups=over_z(at)).astype(F32)


def adamw(weight, grad, first, second, rate, decay, count):
    first_new = BETA_ONE * first + (1.0 - BETA_ONE) * grad
    second_new = BETA_TWO * second + (1.0 - BETA_TWO) * grad * grad
    first_fix = 1.0 - BETA_ONE**count
    second_fix = 1.0 - BETA_TWO**count
    update = first_new / first_fix / (jnp.sqrt(second_new / second_fix) + ADAM_EPS)
    return (weight - rate * (update + decay * weight), first_new, second_new)


def on_device(
    nd,
    nb,
    inputs,
    segments,
    out_grad,
    layer_params,
    attend_weight,
    attend_bias,
    output_weight,
    expand_weight,
    expand_bias,
    shrink_weight,
    mean_layer,
    mean_attend_weight,
    mean_attend_bias,
    mean_output_weight,
    mean_expand_weight,
    mean_expand_bias,
    mean_shrink_weight,
    square_layer,
    square_attend_weight,
    square_attend_bias,
    square_output_weight,
    square_expand_weight,
    square_expand_bias,
    square_shrink_weight,
):
    at = Place(nd, nb)
    x0 = at.x == 0
    rows, block, d = inputs.shape
    length = segments.shape[1]
    tokens = 2 * rows * length
    heads2 = attend_weight.shape[2] // 2
    hidden2 = expand_weight.shape[1] // 2
    gain, shift, out_bias = layer_params[0], layer_params[1], layer_params[2]

    data = inputs.astype(F32)
    center = data - jnp.mean(data, -1, keepdims=True)
    inverse = lax.rsqrt(jnp.mean(center * center, -1, keepdims=True) + EPS_NORM)
    normal = center * inverse
    normed = (normal * gain + shift).astype(LOW)

    def halves(h):
        cols = lambda w: lax.dynamic_slice_in_dim(w, h * heads2, heads2, w.ndim - 1)
        att = attend_weight.astype(LOW)
        attend = jnp.concatenate(
            [cols(att[0]), cols(att[1]), cols(att[2]),
             lax.dynamic_slice_in_dim(output_weight.astype(LOW), h * heads2, heads2, 0).T], 1)
        expand = lax.dynamic_slice_in_dim(expand_weight.astype(LOW), h * hidden2, hidden2, 1)
        shrink = lax.dynamic_slice_in_dim(shrink_weight.astype(LOW), h * hidden2, hidden2, 0).T
        return attend, expand, shrink

    own, away = halves(at.x), halves(1 - at.x)
    pack = jnp.where(x0, jnp.stack([own[0], away[0]]), jnp.stack([away[0], own[0]]))
    biases = jnp.concatenate([attend_bias.reshape(-1), expand_bias]).astype(LOW)
    n_bias = biases.size
    biases = jnp.pad(biases, (0, -n_bias % 128)).reshape(1, -1)
    tok, dy, attend, biases, segs = head(at.nz, nb, normed, out_grad, pack, biases, segments)
    tok, dy = tok.reshape(tokens, d), dy.reshape(tokens, d)
    segs = segs.reshape(2 * rows, length)
    attend = attend.reshape(d, 4 * heads2)
    whole = []
    for mine, theirs in zip(own[1:], away[1:]):
        got = at.swap_x(theirs)
        chunk = jnp.where(x0, jnp.concatenate([mine, got]), jnp.concatenate([got, mine]))
        whole.append(gather_z(at, chunk))
    expand, shrink = whole
    biases = biases[:, 0, :n_bias]
    n_att = attend_bias.shape[1]
    bias_att = jnp.moveaxis(biases[:, : 3 * n_att].reshape(nd, 3, n_att), 0, 1).reshape(3, -1)
    bias_att = lax.dynamic_slice_in_dim(bias_att, at.x * heads2, heads2, 1).astype(F32)
    bias_exp = lax.dynamic_slice_in_dim(
        biases[:, 3 * n_att:].reshape(-1), at.x * hidden2, hidden2, 0).astype(F32)

    att_w, wo_t = attend[:, : 3 * heads2], attend[:, 3 * heads2:]
    proj = dot(tok, att_w, ((1,), (0,))) + bias_att.reshape(-1)
    d_context = dot(dy, wo_t, ((1,), (0,)), LOW)
    context, d_query, d_key, d_value = attention(proj, d_context, segs)
    d_proj = jnp.concatenate([d_query, d_key, d_value], 1)

    up = dot(tok, expand, ((1,), (0,))) + bias_exp
    act, slope = gelu_parts(up)
    act = act.astype(LOW)
    d_up = (dot(dy, shrink, ((1,), (0,))) * slope).astype(LOW)

    grad_attend = jnp.concatenate(
        [dot(tok, d_proj, ((0,), (0,)), LOW), dot(dy, context, ((0,), (0,)), LOW)], 1)
    grad_shrink = dot(dy, act, ((0,), (0,)), LOW)
    grad_expand = dot(tok, d_up, ((0,), (0,)), LOW)

    def owned(part):
        total = scatter_z(at, part)
        total = total.reshape(2, total.shape[0] // 2, total.shape[1])
        pick = lambda i: lax.dynamic_index_in_dim(total, i, 0, keepdims=False)
        mine = pick(at.x)
        got = at.swap_x(pick(1 - at.x).astype(LOW)).astype(F32)
        return jnp.where(x0, mine, got), jnp.where(x0, got, mine)

    lo_a, hi_a = owned(grad_attend)
    lo_s, hi_s = owned(grad_shrink)
    lo_e, hi_e = owned(grad_expand)
    join = lambda i: jnp.concatenate(
        [lo_a[:, i * heads2:(i + 1) * heads2], hi_a[:, i * heads2:(i + 1) * heads2]], 1)
    g_attend = jnp.stack([join(0), join(1), join(2)])
    g_output = join(3).T
    g_expand = jnp.concatenate([lo_e, hi_e], 1)
    g_shrink = jnp.concatenate([lo_s, hi_s], 1).T

    partial = dot(act, shrink, ((1,), (1,))) + dot(context, wo_t, ((1,), (1,)))
    partial = partial.astype(LOW).reshape(2, rows, nb, block, d)
    summed = scatter_tokens(at, partial)
    result = (data + summed + out_bias).astype(LOW)

    partial = dot(d_up, expand, ((1,), (1,))) + dot(d_proj, att_w, ((1,), (1,)))
    partial = partial.astype(LOW).reshape(2, rows, nb, block, d)
    d_normed = scatter_tokens(at, partial)
    grad_gain = jnp.sum(d_normed * normal, (0, 1))
    grad_shift = jnp.sum(d_normed, (0, 1))
    d_normal = d_normed * gain
    d_rows = inverse * (
        d_normal
        - jnp.mean(d_normal, -1, keepdims=True)
        - normal * jnp.mean(d_normal * normal, -1, keepdims=True)
    )
    back = out_grad.astype(F32)
    d_rows = (d_rows + back).astype(LOW)

    small = jnp.stack([grad_gain, grad_shift, jnp.sum(back, (0, 1))])
    pieces = (lo_a, hi_a, lo_s, hi_s, lo_e, hi_e)
    squares = sum(jnp.sum(piece * piece) for piece in pieces)
    bias = jnp.concatenate([jnp.sum(d_proj.astype(F32), 0), jnp.sum(d_up.astype(F32), 0)])
    g_small, bias, bias_other, squares = sums(at.nz, nb, small, bias, squares)
    both = jnp.where(x0, jnp.stack([bias, bias_other]), jnp.stack([bias_other, bias]))
    n_exp = expand_bias.shape[0]
    full_att = jnp.moveaxis(both[:, : 3 * heads2].reshape(2, 3, heads2), 0, 1).reshape(3, 2 * heads2)
    g_bias_att = lax.dynamic_slice_in_dim(full_att, at.dp * n_att, n_att, 1)
    g_bias_exp = lax.dynamic_slice_in_dim(both[:, 3 * heads2:].reshape(-1), at.dp * n_exp, n_exp, 0)

    norm_value = jnp.sqrt(squares + jnp.sum(g_small * g_small))
    size = 4 * d * d + 2 * d * 2 * hidden2 * nb
    factor = jnp.minimum(1.0, math.sqrt(size) / norm_value)
    count = float(STEP)
    params = (layer_params, attend_weight, attend_bias, output_weight, expand_weight, expand_bias, shrink_weight)
    grads = (g_small, g_attend, g_bias_att, g_output, g_expand, g_bias_exp, g_shrink)
    firsts = (mean_layer, mean_attend_weight, mean_attend_bias, mean_output_weight, mean_expand_weight,
              mean_expand_bias, mean_shrink_weight)
    seconds = (square_layer, square_attend_weight, square_attend_bias, square_output_weight,
               square_expand_weight, square_expand_bias, square_shrink_weight)
    is_matrix = (False, True, False, True, True, False, True)
    weights_new, firsts_new, seconds_new = ([], [], [])
    for weight, grad, first, second, matrix in zip(params, grads, firsts, seconds, is_matrix):
        rate = MATRIX_RATE if matrix else VECTOR_RATE
        decay = DECAY if matrix else 0.0
        new = adamw(weight, factor * grad, first, second, rate, decay, count)
        weights_new.append(new[0])
        firsts_new.append(new[1])
        seconds_new.append(new[2])
    return (
        result,
        d_rows,
        norm_value.reshape(1),
        *weights_new,
        *firsts_new,
        *seconds_new,
        weights_new[1].astype(LOW),
        weights_new[3].astype(LOW),
        weights_new[4].astype(LOW),
        weights_new[6].astype(LOW),
    )


def solution(mesh):
    nd, nb = mesh.shape["dp"], mesh.shape["branch"]
    state = (
        P(),
        P(None, "dp", "branch"),
        P(None, ("branch", "dp")),
        P("branch", "dp"),
        P("dp", "branch"),
        P(("branch", "dp")),
        P("branch", "dp"),
    )
    rows = P("dp", "branch", None)
    return jax.shard_map(
        lambda *args: on_device(nd, nb, *args),
        mesh=mesh,
        in_specs=(rows, P("dp", None), rows) + state * 3,
        out_specs=(rows, rows, P()) + state * 3 + (state[1], state[3], state[4], state[6]),
        check_vma=False,
    )
```
